128 devices in a mesh: src: 16 (over y_hi, z, core), tgt: 8 (over y_lo, x).
Axes of the slice: x: 4, y: 4 (y_hi: 2, y_lo: 2; y = y_hi * 2 + y_lo), z: 4, core: 2. Of those that a mesh axis runs over, the one named last changes fastest.
Arguments:
- sources: float32 [64, 128, 16384], P(None, None, ('src', 'tgt')), may hold values from -6 to 6
- source_interp: float32 [128, 32, 16384], P(None, None, ('src', 'tgt')), may hold values from -0.5 to 0.5
- target_interp: float32 [128, 32, 16384], P(None, None, ('src', 'tgt')), may hold values from -1 to 1
- transfer: float32 [9, 32, 64, 16384], P(None, None, None, ('src', 'tgt')), may hold values from -0.75 to 0.75
Outputs:
- targets: float32 [64, 128, 16384], P(None, None, ('src', 'tgt'))
The draws below stay inside these ranges and needn't reach their ends.
All inputs are finite; a program needn't handle non-finite values.
Results may differ from the reference program's by a relative error of at most 0.00017.
Values sent between devices are 32-bit elements; how exact they have to be, the bound alone decides.
No kernel may reach another device: no remote copies, remote signals or barrier semaphores. Data moves between devices by JAX's collectives and lax.ppermute only.
A program may use at most 128 MiB of HBM per device.

```python
import jax
import jax.numpy as jnp
from jax import lax

K = 32
R = 64
B = 128
LOCAL_LEVELS = 2
LEVELS = 9
NB = 16384
N_SRC = 16
N_TGT = 8


def shard_levels(rng, shape, cuts, least, top_value):
    def one(dim, parts):
        steps = jax.random.uniform(jax.random.fold_in(jax.random.fold_in(rng, 6), dim), (parts,), jnp.float32, least / len(cuts), top_value / len(cuts))
        return jnp.repeat(jnp.exp(steps), shape[dim] // parts).reshape((-1,) + (1,) * (len(shape) - dim - 1))

    level = one(*cuts[0])
    for cut in cuts[1:]:
        level = level * one(*cut)
    return level


def noise(key, shape, deviation, reach, cuts=(), held_as=jnp.bfloat16):
    drawn = deviation * jax.random.normal(key, shape, jnp.float32)
    if cuts:
        drawn = drawn * shard_levels(key, shape, cuts, -0.22, 0.18)
    return jnp.clip(drawn, -reach, reach).astype(held_as)


def setup_inputs(seed: int = 0) -> dict:
    keys = jax.random.split(jax.random.key(seed), 5)
    return {
        "sources": noise(keys[0], (R, B, NB), 1.0, 6.0, ((2, 128),), jnp.float32),
        "source_interp": noise(keys[1], (B, K, NB), B ** -0.5, 0.5, ((2, 128),), jnp.float32),
        "target_interp": noise(keys[2], (B, K, NB), K ** -0.5, 1.0, ((2, 128),), jnp.float32),
        "transfer": noise(keys[3], (LEVELS, K, 2 * K, NB), (2 * K) ** -0.5, 0.75, ((3, 128),), jnp.float32),
    }


def flip_axis(values, axis, half):
    shape = values.shape
    length = shape[axis]
    split = shape[:axis] + (length // (2 * half), 2, half) + shape[axis + 1:]
    return jnp.flip(values.reshape(split), axis + 1).reshape(shape)


def mixing(weight, coeffs):
    return jnp.einsum('kjg,jrg->krg', weight, coeffs, precision=lax.Precision.HIGHEST)


def reference(sources, source_interp, target_interp, transfer):
    rank = source_interp.shape[1]
    blocks_dev = sources.shape[2] // (N_SRC * N_TGT)
    local_bits = blocks_dev.bit_length() - 1
    src_bits = N_SRC.bit_length() - 1
    tgt_bits = N_TGT.bit_length() - 1
    order = [m for m in range(LOCAL_LEVELS)]
    order = order + [local_bits + tgt_bits + j for j in range(src_bits)]
    order = order + [local_bits + j for j in range(tgt_bits)]
    coeffs = jnp.einsum('bkg,rbg->krg', source_interp, sources, precision=lax.Precision.HIGHEST)
    for position, bit_pos in enumerate(order):
        weight = transfer[position]
        partner = flip_axis(coeffs, 2, 1 << bit_pos)
        coeffs = mixing(weight[:, :rank], coeffs) + mixing(weight[:, rank:], partner)
    return jnp.einsum('bkg,krg->rbg', target_interp, coeffs, precision=lax.Precision.HIGHEST)
```

```python
import jax
import jax.numpy as jnp
from jax import lax
from jax.experimental import pallas as pl
from jax.experimental.pallas import tpu as pltpu
from jax.sharding import PartitionSpec as P

R, B, K, NB = 64, 128, 32, 128
HALF = NB // 2
CHUNKS = (16, 16, 16, 16)
MIB = 1 << 20
F32, BF16 = jnp.float32, jnp.bfloat16
VMEM = pl.BlockSpec(memory_space=pltpu.VMEM)


def in_vmem(*arrays):
    return [pltpu.with_memory_space_constraint(x, pltpu.VMEM) for x in arrays]


def in_hbm(*arrays):
    return [pltpu.with_memory_space_constraint(x, pltpu.HBM) for x in arrays]


def split(x):
    high = x.astype(BF16)
    return high, (x - high.astype(F32)).astype(BF16)


def low_lanes(shape):
    return lax.broadcasted_iota(jnp.int32, shape, len(shape) - 1) < HALF


def prepare_transfer(block, out_ref, k0):
    turned = [jnp.concatenate([block[i], block[i + 8]], 0).T for i in range(8)]
    mask = low_lanes((8, 8, NB))
    for g0 in range(0, NB, 8):
        v = jnp.swapaxes(jnp.stack([t[g0 : g0 + 8] for t in turned]), 0, 1)
        w = pltpu.roll(v, HALF, 2)
        vh = v.astype(BF16).astype(F32)
        wh = w.astype(BF16).astype(F32)
        first = jnp.where(mask, vh, w - wh)
        second = jnp.where(mask, wh, v - vh)
        gh, gl = divmod(g0, HALF)
        rows = jnp.concatenate([first, second], 1).astype(BF16)
        out_ref[gl : gl + 8, gh * K + k0 : gh * K + k0 + 16, :] = rows


def mix(weight, own, partner, mask):
    high, low = split(jnp.concatenate([own, partner], 0))
    both = jnp.concatenate([weight, weight], 1)
    s = jnp.dot(both, jnp.concatenate([high, high, low, low], 0), preferred_element_type=F32)
    return jnp.where(mask, s[:K], s[K:])


def source_kernel(src_ref, si_ref, t_ref, *refs):
    n = len(CHUNKS)
    outs, (s_ref, a_ref, m_ref, t0_ref, t1_ref, c_ref, d_ref) = refs[:n], refs[n:]
    step = pl.program_id(0)

    turned = [src_ref[i].T for i in range(8)]
    r0 = pl.multiple_of(step * 8, 8)
    for g0 in range(0, NB, 8):
        v = jnp.swapaxes(jnp.stack([t[g0 : g0 + 8] for t in turned]), 0, 1)
        s_ref[g0 : g0 + 8, pl.ds(r0, 8), :] = v
    b0 = pl.multiple_of(step * 16, 8)
    for i in range(2):
        a_ref[:, pl.ds(pl.multiple_of(b0 + 8 * i, 8), 8), :] = jnp.swapaxes(si_ref[8 * i : 8 * i + 8], 0, 1)

    for s in range(4):
        @pl.when(step == s)
        def _():
            prepare_transfer(t_ref[0], t0_ref if s < 2 else t1_ref, 16 * (s % 2))

    @pl.when(step == 7)
    def _():
        @pl.loop(0, K // 8)
        def _(i):
            k0 = pl.multiple_of(i * 8, 8)
            turned = [a_ref[k0 + j].T for j in range(8)]
            for g0 in range(0, NB, 8):
                v = jnp.swapaxes(jnp.stack([t[g0 : g0 + 8] for t in turned]), 0, 1)
                m_ref[g0 : g0 + 8, pl.ds(k0, 8), :] = v

        mask = low_lanes((K, NB))

        @pl.loop(0, 4)
        def _(i):
            for j in range(16):
                gl = i * 16 + j
                mh, ml = split(jnp.concatenate([m_ref[gl], m_ref[gl + HALF]], 0))
                sh, sl = split(jnp.concatenate([s_ref[gl], s_ref[gl + HALF]], 0))
                dims = (((1,), (1,)), ((), ()))
                s = lax.dot_general(jnp.concatenate([mh, ml], 1), jnp.concatenate([sh, sh], 1), dims, preferred_element_type=F32)
                s = s + lax.dot_general(mh, sl, dims, preferred_element_type=F32)
                c_ref[gl] = jnp.where(mask, s[:K], s[K:])

        @pl.loop(0, 4)
        def _(i):
            for j in range(16):
                d_ref[i * 16 + j] = mix(t0_ref[i * 16 + j], c_ref[i * 16 + j], c_ref[i * 16 + (j ^ 1)], mask)

        first = 0
        for out, size in zip(outs, CHUNKS):
            for j in range(size):
                gl = first + j
                out[j] = mix(t1_ref[gl], d_ref[gl], d_ref[gl ^ 2], mask)
            first += size


def source_stage(sources, source_interp, transfer):
    return pl.pallas_call(
        source_kernel,
        name="source_stage",
        grid=(8,),
        in_specs=[
            pl.BlockSpec((8, B, NB), lambda i: (i, 0, 0)),
            pl.BlockSpec((16, K, NB), lambda i: (i, 0, 0)),
            pl.BlockSpec((1, 16, 2 * K, NB), lambda i: (jnp.minimum(i // 2, 1), jnp.where(i < 4, i % 2, 1), 0, 0)),
        ],
        out_specs=[VMEM] * len(CHUNKS),
        out_shape=[pltpu.VMEM((size, K, NB), F32) for size in CHUNKS],
        scratch_shapes=[
            pltpu.VMEM((NB, R, B), F32),
            pltpu.VMEM((K, B, NB), F32),
            pltpu.VMEM((NB, K, B), F32),
            pltpu.VMEM((HALF, 2 * K, NB), BF16),
            pltpu.VMEM((HALF, 2 * K, NB), BF16),
            pltpu.VMEM((HALF, K, NB), F32),
            pltpu.VMEM((HALF, K, NB), F32),
        ],
        compiler_params=pltpu.CompilerParams(vmem_limit_bytes=20 * MIB),
    )(*in_hbm(sources, source_interp, transfer))


def transfer_stage(transfer, level):
    def kernel(t_ref, o_ref):
        for i in range(2):
            prepare_transfer(t_ref.at[level, pl.ds(16 * i, 16)], o_ref, 16 * i)

    return pl.pallas_call(
        kernel,
        name=f"transfer_{level}",
        in_specs=[VMEM],
        out_specs=VMEM,
        out_shape=pltpu.VMEM((HALF, 2 * K, NB), BF16),
        compiler_params=pltpu.CompilerParams(vmem_limit_bytes=4 * MIB),
        cost_estimate=pl.CostEstimate(flops=10**6, bytes_accessed=4 * MIB, transcendentals=0),
    )(*in_vmem(transfer))


def target_matrix_kernel(ti_ref, o_ref, a_ref):
    for b0 in range(0, B, 8):
        a_ref[:, b0 : b0 + 8, :] = jnp.swapaxes(ti_ref[b0 : b0 + 8], 0, 1)

    @pl.loop(0, K // 8)
    def _(i):
        k0 = pl.multiple_of(i * 8, 8)
        turned = [a_ref[k0 + j].T for j in range(8)]
        for g0 in range(0, NB, 8):
            v = jnp.swapaxes(jnp.stack([t[g0 : g0 + 8] for t in turned]), 0, 1)
            o_ref[g0 : g0 + 8, pl.ds(k0, 8), :] = v


def target_matrix_stage(target_interp):
    return pl.pallas_call(
        target_matrix_kernel,
        name="target_matrix",
        in_specs=[VMEM],
        out_specs=VMEM,
        out_shape=pltpu.VMEM((NB, K, B), F32),
        scratch_shapes=[pltpu.VMEM((K, B, NB), F32)],
        compiler_params=pltpu.CompilerParams(vmem_limit_bytes=6 * MIB),
        cost_estimate=pl.CostEstimate(flops=10**6, bytes_accessed=8 * MIB, transcendentals=0),
    )(*in_vmem(target_interp))


def level_stage(weights, own, partner, first, level):
    size = own.shape[0]

    def kernel(t_ref, c_ref, p_ref, o_ref):
        mask = low_lanes((K, NB))
        for j in range(size):
            o_ref[j] = mix(t_ref[first + j], c_ref[j], p_ref[j], mask)

    return pl.pallas_call(
        kernel,
        name=f"level_{level}_{first}",
        in_specs=[VMEM] * 3,
        out_specs=VMEM,
        out_shape=pltpu.VMEM((size, K, NB), F32),
        compiler_params=pltpu.CompilerParams(vmem_limit_bytes=2 * MIB),
        cost_estimate=pl.CostEstimate(flops=size * 2 * 64 * 256 * 128, bytes_accessed=size * 64 * 1024, transcendentals=0),
    )(*in_vmem(weights, own, partner))


def last_stage(weights, own, partner, matrix, first):
    size = own.shape[0]

    def kernel(t_ref, c_ref, p_ref, m_ref, o_ref):
        mask = low_lanes((K, NB))
        for j0 in range(0, size, 8):
            values = [[], []]
            for j in range(j0, j0 + 8):
                gl = first + j
                c = mix(t_ref[gl], c_ref[j], p_ref[j], mask)
                high, low = split(c)
                left = jnp.concatenate([high, low, high, low], 0).T
                for gh in range(2):
                    th, tl = split(m_ref[gh * HALF + gl])
                    right = jnp.concatenate([th, th, tl, tl], 0)
                    values[gh].append(jnp.dot(left[gh * R : gh * R + R], right, preferred_element_type=F32))
            for gh in range(2):
                o_ref[:, gh, j0 : j0 + 8, :] = jnp.swapaxes(jnp.stack(values[gh]), 0, 1)

    return pl.pallas_call(
        kernel,
        name=f"last_{first}",
        in_specs=[VMEM] * 4,
        out_specs=VMEM,
        out_shape=pltpu.VMEM((R, 2, size, B), F32),
        compiler_params=pltpu.CompilerParams(vmem_limit_bytes=4 * MIB),
        cost_estimate=pl.CostEstimate(flops=size * 4 * 64 * 256 * 128, bytes_accessed=size * 128 * 1024, transcendentals=0),
    )(*in_vmem(weights, own, partner, matrix))


def output_stage(parts):
    def kernel(*refs):
        *ins, o_ref = refs
        r0 = pl.program_id(0) * 8
        for i in range(8):
            rows = [ref[r0 + i, gh] for gh in range(2) for ref in ins]
            o_ref[i] = jnp.concatenate(rows, 0).T

    return pl.pallas_call(
        kernel,
        name="output",
        grid=(8,),
        in_specs=[VMEM] * len(parts),
        out_specs=pl.BlockSpec((8, B, NB), lambda i: (i, 0, 0)),
        out_shape=jax.ShapeDtypeStruct((R, B, NB), F32),
        compiler_params=pltpu.CompilerParams(vmem_limit_bytes=4 * MIB),
    )(*in_vmem(*parts))


def device_program(exchange, sources, source_interp, target_interp, transfer):
    chunks = source_stage(sources, source_interp, transfer)
    firsts = [sum(CHUNKS[:i]) for i in range(len(CHUNKS))]
    for level in range(2, 8):
        weights = transfer_stage(transfer, level)
        partners = [exchange(c, level) for c in chunks]
        chunks = [level_stage(weights, c, p, first, level) for c, p, first in zip(chunks, partners, firsts)]
    weights = transfer_stage(transfer, 8)
    matrix = target_matrix_stage(target_interp)
    partners = [exchange(c, 8) for c in chunks]
    parts = [last_stage(weights, c, p, matrix, first) for c, p, first in zip(chunks, partners, firsts)]
    return output_stage(parts)


def solution(mesh):
    n_src, n_tgt = mesh.shape["src"], mesh.shape["tgt"]

    def exchange(c, level):
        if level < 6:
            axis, size, bit = "src", n_src, level - 2
        else:
            axis, size, bit = "tgt", n_tgt, level - 6
        return lax.ppermute(c, axis, [(i, i ^ (1 << bit)) for i in range(size)])

    def program(*args):
        return device_program(exchange, *args)

    blocks = ("src", "tgt")
    return jax.shard_map(
        program,
        mesh=mesh,
        in_specs=(P(None, None, blocks), P(None, None, blocks), P(None, None, blocks), P(None, None, None, blocks)),
        out_specs=P(None, None, blocks),
        check_vma=False,
    )
```

```python
import jax
import jax.numpy as jnp
from jax import lax
from jax.experimental import pallas as pl
from jax.experimental.pallas import tpu as pltpu
from jax.sharding import PartitionSpec as P

R, B, K, NB = 64, 128, 32, 128
HALF = NB // 2
CHUNKS = (16, 16, 16, 16)
MIB = 1 << 20
F32, BF16 = jnp.float32, jnp.bfloat16
VMEM = pl.BlockSpec(memory_space=pltpu.VMEM)
ANY = pl.BlockSpec(memory_space=pl.ANY)
NEAR_ZERO = pl.CostEstimate(flops=1, bytes_accessed=1, transcendentals=0)
STEP = (0, 1, -2, 0, 1, -3, -4, -5, -6, -7, -8, -9, 0, 2, 1, 3, 0, 2, 1, 3, 0, 2, 1, 3, 0, 2, 1, 3, 0, 2, 1, 3, 0, 2, 1, 3, 2, 3, 2, 3)
ORDER = [("step", i) if i >= 0 else ("prepare", -i) for i in STEP]


def in_vmem(*arrays):
    return [pltpu.with_memory_space_constraint(x, pltpu.VMEM) for x in arrays]


def in_hbm(*arrays):
    return [pltpu.with_memory_space_constraint(x, pltpu.HBM) for x in arrays]


def split(x):
    high = x.astype(BF16)
    return high, (x - high.astype(F32)).astype(BF16)


def low_lanes(shape):
    return lax.broadcasted_iota(jnp.int32, shape, len(shape) - 1) < HALF


def prepare_transfer(block, out_ref, k0):
    turned = [jnp.concatenate([block[i], block[i + 8]], 0).T for i in range(8)]
    mask = low_lanes((8, 8, NB))
    for g0 in range(0, NB, 8):
        v = jnp.swapaxes(jnp.stack([t[g0 : g0 + 8] for t in turned]), 0, 1)
        w = pltpu.roll(v, HALF, 2)
        vh = v.astype(BF16).astype(F32)
        wh = w.astype(BF16).astype(F32)
        first = jnp.where(mask, vh, w - wh)
        second = jnp.where(mask, wh, v - vh)
        gh, gl = divmod(g0, HALF)
        rows = jnp.concatenate([first, second], 1).astype(BF16)
        out_ref[gl : gl + 8, gh * K + k0 : gh * K + k0 + 16, :] = rows


def mix(weight, own, partner, mask):
    high, low = split(jnp.concatenate([own, partner], 0))
    both = jnp.concatenate([weight, weight], 1)
    s = jnp.dot(both, jnp.concatenate([high, high, low, low], 0), preferred_element_type=F32)
    return jnp.where(mask, s[:K], s[K:])


def source_prepare(sources, source_interp, transfer):
    def kernel(src_hbm, si_hbm, t_hbm, s_ref, m_ref, t0_ref, t1_ref, src, si, t, a_ref, src_sem, si_sem, t_sem):
        si_copy = [pltpu.make_async_copy(si_hbm.at[pl.ds(32 * i, 32)], si.at[pl.ds(32 * i, 32)], si_sem.at[i]) for i in range(4)]
        t_copy = [pltpu.make_async_copy(t_hbm.at[i], t.at[i], t_sem.at[i]) for i in range(2)]

        def src_copy(i):
            rows = pl.ds(pl.multiple_of(8 * i, 8), 8)
            return pltpu.make_async_copy(src_hbm.at[rows], src.at[rows], src_sem.at[i])

        for copy in si_copy + [src_copy(i) for i in range(8)] + t_copy:
            copy.start()
        for i in range(4):
            si_copy[i].wait()
            for b0 in range(32 * i, 32 * i + 32, 8):
                a_ref[:, b0 : b0 + 8, :] = jnp.swapaxes(si[b0 : b0 + 8], 0, 1)

        def turn(block, out_ref, first):
            turned = [block(j).T for j in range(8)]
            for g0 in range(0, NB, 8):
                out_ref[g0 : g0 + 8, pl.ds(first, 8), :] = jnp.swapaxes(jnp.stack([x[g0 : g0 + 8] for x in turned]), 0, 1)

        @pl.loop(0, K // 8)
        def _(i):
            k0 = pl.multiple_of(i * 8, 8)
            turn(lambda j: a_ref[k0 + j], m_ref, k0)

        @pl.loop(0, 8)
        def _(i):
            src_copy(i).wait()
            r0 = pl.multiple_of(i * 8, 8)
            turn(lambda j: src[r0 + j], s_ref, r0)

        for i, out_ref in enumerate((t0_ref, t1_ref)):
            t_copy[i].wait()
            for half in range(2):
                prepare_transfer(t.at[i, pl.ds(16 * half, 16)], out_ref, 16 * half)

    hbm = pl.BlockSpec(memory_space=pltpu.HBM)
    return pl.pallas_call(
        kernel,
        name="source_prepare",
        in_specs=[hbm] * 3,
        out_specs=[VMEM] * 4,
        out_shape=[pltpu.VMEM((NB, R, B), F32), pltpu.VMEM((NB, K, B), F32)] + [pltpu.VMEM((HALF, 2 * K, NB), BF16)] * 2,
        scratch_shapes=[
            pltpu.VMEM((R, B, NB), F32),
            pltpu.VMEM((B, K, NB), F32),
            pltpu.VMEM((2, K, 2 * K, NB), F32),
            pltpu.VMEM((K, B, NB), F32),
            pltpu.SemaphoreType.DMA((8,)),
            pltpu.SemaphoreType.DMA((4,)),
            pltpu.SemaphoreType.DMA((2,)),
        ],
        compiler_params=pltpu.CompilerParams(vmem_limit_bytes=14 * MIB),
    )(*in_hbm(sources, source_interp, transfer))


def source_stage(prepared, first, size, after):
    def kernel(s_ref, m_ref, t0_ref, t1_ref, _, o_ref, c_ref, d_ref):
        mask = low_lanes((K, NB))
        dims = (((1,), (1,)), ((), ()))
        for j in range(size):
            gl = first + j
            mh, ml = split(jnp.concatenate([m_ref[gl], m_ref[gl + HALF]], 0))
            sh, sl = split(jnp.concatenate([s_ref[gl], s_ref[gl + HALF]], 0))
            s = lax.dot_general(jnp.concatenate([mh, ml], 1), jnp.concatenate([sh, sh], 1), dims, preferred_element_type=F32)
            s = s + lax.dot_general(mh, sl, dims, preferred_element_type=F32)
            c_ref[j] = jnp.where(mask, s[:K], s[K:])
        for j in range(size):
            d_ref[j] = mix(t0_ref[first + j], c_ref[j], c_ref[j ^ 1], mask)
        for j in range(size):
            o_ref[j] = mix(t1_ref[first + j], d_ref[j], d_ref[j ^ 2], mask)

    return pl.pallas_call(
        kernel,
        name=f"source_{first}",
        in_specs=[VMEM] * 4 + [ANY],
        out_specs=VMEM,
        out_shape=pltpu.VMEM((size, K, NB), F32),
        scratch_shapes=[pltpu.VMEM((size, K, NB), F32)] * 2,
        compiler_params=pltpu.CompilerParams(vmem_limit_bytes=4 * MIB),
        cost_estimate=NEAR_ZERO,
    )(*in_vmem(*prepared, after))


def transfer_stage(transfer, level, after):
    def kernel(t_ref, _, o_ref):
        for i in range(2):
            prepare_transfer(t_ref.at[level, pl.ds(16 * i, 16)], o_ref, 16 * i)

    return pl.pallas_call(
        kernel,
        name=f"transfer_{level}",
        in_specs=[VMEM, ANY],
        out_specs=VMEM,
        out_shape=pltpu.VMEM((HALF, 2 * K, NB), BF16),
        compiler_params=pltpu.CompilerParams(vmem_limit_bytes=4 * MIB),
        cost_estimate=NEAR_ZERO,
    )(*in_vmem(transfer, after))


def target_matrix_kernel(ti_ref, _, o_ref, a_ref):
    for b0 in range(0, B, 8):
        a_ref[:, b0 : b0 + 8, :] = jnp.swapaxes(ti_ref[b0 : b0 + 8], 0, 1)

    @pl.loop(0, K // 8)
    def _(i):
        k0 = pl.multiple_of(i * 8, 8)
        turned = [a_ref[k0 + j].T for j in range(8)]
        for g0 in range(0, NB, 8):
            v = jnp.swapaxes(jnp.stack([t[g0 : g0 + 8] for t in turned]), 0, 1)
            o_ref[g0 : g0 + 8, pl.ds(k0, 8), :] = v


def target_matrix_stage(target_interp, after):
    return pl.pallas_call(
        target_matrix_kernel,
        name="target_matrix",
        in_specs=[VMEM, ANY],
        out_specs=VMEM,
        out_shape=pltpu.VMEM((NB, K, B), F32),
        scratch_shapes=[pltpu.VMEM((K, B, NB), F32)],
        compiler_params=pltpu.CompilerParams(vmem_limit_bytes=6 * MIB),
        cost_estimate=NEAR_ZERO,
    )(*in_vmem(target_interp, after))


def level_stage(weights, own, partner, first, level, after):
    size = own.shape[0]

    def kernel(t_ref, c_ref, p_ref, _, o_ref):
        mask = low_lanes((K, NB))
        for j in range(size):
            o_ref[j] = mix(t_ref[first + j], c_ref[j], p_ref[j], mask)

    return pl.pallas_call(
        kernel,
        name=f"level_{level}_{first}",
        in_specs=[VMEM] * 3 + [ANY],
        out_specs=VMEM,
        out_shape=pltpu.VMEM((size, K, NB), F32),
        compiler_params=pltpu.CompilerParams(vmem_limit_bytes=2 * MIB),
        cost_estimate=NEAR_ZERO,
    )(*in_vmem(weights, own, partner, after))


def last_stage(weights, own, partner, matrix, first, after):
    size = own.shape[0]

    def kernel(t_ref, c_ref, p_ref, m_ref, _, o_ref, d_ref, v_ref):
        mask = low_lanes((K, NB))
        for j in range(size):
            d_ref[j] = mix(t_ref[first + j], c_ref[j], p_ref[j], mask)
        for j in range(size):
            gl = first + j
            high, low = split(d_ref[j])
            left = jnp.concatenate([high, low, high, low], 0).T
            for gh in range(2):
                th, tl = split(m_ref[gh * HALF + gl])
                right = jnp.concatenate([th, th, tl, tl], 0)
                v_ref[gh, j] = jnp.dot(left[gh * R : gh * R + R], right, preferred_element_type=F32)
        for gh in range(2):
            for j0 in range(0, size, 8):
                for r0 in range(0, R, 8):
                    o_ref[r0 : r0 + 8, gh, j0 : j0 + 8, :] = jnp.swapaxes(v_ref[gh, j0 : j0 + 8, r0 : r0 + 8, :], 0, 1)

    return pl.pallas_call(
        kernel,
        name=f"last_{first}",
        in_specs=[VMEM] * 4 + [ANY],
        out_specs=VMEM,
        out_shape=pltpu.VMEM((R, 2, size, B), F32),
        scratch_shapes=[pltpu.VMEM((size, K, NB), F32), pltpu.VMEM((2, size, R, B), F32)],
        compiler_params=pltpu.CompilerParams(vmem_limit_bytes=4 * MIB),
        cost_estimate=NEAR_ZERO,
    )(*in_vmem(weights, own, partner, matrix, after))


def output_stage(parts):
    def kernel(*refs):
        ins, (o_hbm, o_ref, sem) = refs[:-3], refs[-3:]

        def copy(i):
            rows = pl.ds(pl.multiple_of(8 * i, 8), 8)
            return pltpu.make_async_copy(o_ref.at[rows], o_hbm.at[rows], sem.at[i])

        @pl.loop(0, 8)
        def _(i):
            for j in range(8):
                r = i * 8 + j
                o_ref[r] = jnp.concatenate([ref[r, gh] for gh in range(2) for ref in ins], 0).T
            copy(i).start()

        @pl.loop(0, 8)
        def _(i):
            copy(i).wait()

    return pl.pallas_call(
        kernel,
        name="output",
        in_specs=[VMEM] * len(parts),
        out_specs=pl.BlockSpec(memory_space=pltpu.HBM),
        out_shape=pltpu.HBM((R, B, NB), F32),
        scratch_shapes=[pltpu.VMEM((R, B, NB), F32), pltpu.SemaphoreType.DMA((8,))],
        compiler_params=pltpu.CompilerParams(vmem_limit_bytes=6 * MIB),
    )(*in_vmem(*parts))


def device_program(exchange, sources, source_interp, target_interp, transfer):
    prepared = source_prepare(sources, source_interp, transfer)
    count = len(CHUNKS)
    firsts = [sum(CHUNKS[:i]) for i in range(count)]
    weights, parts = {}, {}
    level, own, partner = [1] * count, [None] * count, [None] * count
    after = prepared[2]
    for kind, index in ORDER:
        if kind == "prepare":
            if index == 9:
                after = weights[9] = target_matrix_stage(target_interp, after)
            else:
                after = weights[index] = transfer_stage(transfer, index, after)
            continue
        first, size, n = firsts[index], CHUNKS[index], level[index]
        if n == 8:
            after = parts[index] = last_stage(weights[8], own[index], partner[index], weights[9], first, after)
            continue
        if n == 1:
            after = source_stage(prepared, first, size, after)
        else:
            after = level_stage(weights[n], own[index], partner[index], first, n, after)
        own[index], level[index] = after, n + 1
        partner[index] = exchange(after, n + 1)
    return output_stage([parts[i] for i in range(count)])


def solution(mesh):
    n_src, n_tgt = mesh.shape["src"], mesh.shape["tgt"]

    def exchange(c, level):
        if level < 6:
            axis, size, bit = "src", n_src, level - 2
        else:
            axis, size, bit = "tgt", n_tgt, level - 6
        return lax.ppermute(c, axis, [(i, i ^ (1 << bit)) for i in range(size)])

    def program(*args):
        return device_program(exchange, *args)

    blocks = ("src", "tgt")
    return jax.shard_map(
        program,
        mesh=mesh,
        in_specs=(P(None, None, blocks), P(None, None, blocks), P(None, None, blocks), P(None, None, None, blocks)),
        out_specs=P(None, None, blocks),
        check_vma=False,
    )
```

```python
import jax
import jax.numpy as jnp
from jax import lax
from jax.experimental import pallas as pl
from jax.experimental.pallas import tpu as pltpu
from jax.sharding import PartitionSpec as P

R, B, K, NB = 64, 128, 32, 128
HALF = NB // 2
CHUNKS = (16, 16, 16, 16)
MIB = 1 << 20
F32, BF16 = jnp.float32, jnp.bfloat16
VMEM = pl.BlockSpec(memory_space=pltpu.VMEM)
ANY = pl.BlockSpec(memory_space=pl.ANY)
NEAR_ZERO = pl.CostEstimate(flops=1, bytes_accessed=1, transcendentals=0)
STEP = (0, 1, 0, 1, -1, -3, -4, -5, -6, -7, 0, 2, 1, 3, -8, 0, 2, 1, 3, 0, 2, 1, -9, 3, 0, 2, 1, 3, 0, 2, 1, 3, 2, 3, 0, 2, 1, 3, 2, 3)
ORDER = [("step", i) if i >= 0 else ("prepare", -i) for i in STEP]


def in_vmem(*arrays):
    return [pltpu.with_memory_space_constraint(x, pltpu.VMEM) for x in arrays]


def in_hbm(*arrays):
    return [pltpu.with_memory_space_constraint(x, pltpu.HBM) for x in arrays]


def split(x):
    high = x.astype(BF16)
    return high, (x - high.astype(F32)).astype(BF16)


def low_lanes(shape):
    return lax.broadcasted_iota(jnp.int32, shape, len(shape) - 1) < HALF


def turn_transfer(block):
    return [jnp.concatenate([block[i], block[i + 8]], 0).T for i in range(8)]


def place_transfer(turned, out_ref, gl, gh, k0):
    mask = low_lanes((8, 8, NB))
    v = jnp.swapaxes(jnp.stack(turned), 0, 1)
    w = pltpu.roll(v, HALF, 2)
    vh = v.astype(BF16).astype(F32)
    wh = w.astype(BF16).astype(F32)
    first = jnp.where(mask, vh, w - wh)
    second = jnp.where(mask, wh, v - vh)
    rows = jnp.concatenate([first, second], 1).astype(BF16)
    out_ref[gl : gl + 8, gh * K + k0 : gh * K + k0 + 16, :] = rows


def prepare_transfer(block, out_ref, k0):
    turned = turn_transfer(block)
    for g0 in range(0, NB, 8):
        gh, gl = divmod(g0, HALF)
        place_transfer([t[g0 : g0 + 8] for t in turned], out_ref, gl, gh, k0)


def mix(weight, own, partner, mask):
    high, low = split(jnp.concatenate([own, partner], 0))
    both = jnp.concatenate([weight, weight], 1)
    s = jnp.dot(both, jnp.concatenate([high, high, low, low], 0), preferred_element_type=F32)
    return jnp.where(mask, s[:K], s[K:])


PART = HALF // 2
EARLY = 3


def part_shapes():
    matrices = [pltpu.VMEM((PART, 2 * K, NB), BF16)] * EARLY
    return [pltpu.VMEM((HALF, R, B), F32), pltpu.VMEM((HALF, K, B), F32)] + matrices


def source_prepare(sources, source_interp, transfer):
    def kernel(src_hbm, si_hbm, t_hbm, s_ref, m_ref, *refs):
        t_refs, (us_ref, um_ref, ut_ref, src, si, t, a_ref, src_sem, si_sem, t_sem) = refs[:EARLY], refs[EARLY:]
        si_copy = [pltpu.make_async_copy(si_hbm.at[pl.ds(32 * i, 32)], si.at[pl.ds(32 * i, 32)], si_sem.at[i]) for i in range(4)]
        t_copy = [pltpu.make_async_copy(t_hbm.at[i], t.at[i], t_sem.at[i]) for i in range(EARLY)]

        def src_copy(i):
            rows = pl.ds(pl.multiple_of(8 * i, 8), 8)
            return pltpu.make_async_copy(src_hbm.at[rows], src.at[rows], src_sem.at[i])

        for copy in si_copy + [src_copy(i) for i in range(8)] + t_copy:
            copy.start()
        for i in range(4):
            si_copy[i].wait()
            for b0 in range(32 * i, 32 * i + 32, 8):
                a_ref[:, b0 : b0 + 8, :] = jnp.swapaxes(si[b0 : b0 + 8], 0, 1)

        def turn(block, out_ref, rest_ref, first):
            turned = [block(j).T for j in range(8)]
            for gh in range(2):
                for q in range(0, PART, 8):
                    g0 = gh * HALF + q
                    rows = jnp.swapaxes(jnp.stack([x[g0 : g0 + 8] for x in turned]), 0, 1)
                    out_ref[gh * PART + q : gh * PART + q + 8, pl.ds(first, 8), :] = rows
                g0 = gh * HALF + PART
                for j in range(8):
                    rest_ref[first + j, gh * PART : gh * PART + PART, :] = turned[j][g0 : g0 + PART]

        @pl.loop(0, K // 8, unroll=True)
        def _(i):
            k0 = pl.multiple_of(i * 8, 8)
            turn(lambda j: a_ref[k0 + j], m_ref, um_ref, k0)

        @pl.loop(0, 8, unroll=True)
        def _(i):
            src_copy(i).wait()
            r0 = pl.multiple_of(i * 8, 8)
            turn(lambda j: src[r0 + j], s_ref, us_ref, r0)

        for i, out_ref in enumerate(t_refs):
            t_copy[i].wait()
            for half in range(2):
                turned = turn_transfer(t.at[i, pl.ds(16 * half, 16)])
                for gh in range(2):
                    for q in range(0, PART, 8):
                        g0 = gh * HALF + q
                        place_transfer([x[g0 : g0 + 8] for x in turned], out_ref, q, gh, 16 * half)
                    g0 = gh * HALF + PART
                    for j in range(8):
                        ut_ref[i, half, j, gh * PART : gh * PART + PART, :] = turned[j][g0 : g0 + PART]

    hbm = pl.BlockSpec(memory_space=pltpu.HBM)
    rest = [pltpu.VMEM((R, HALF, B), F32), pltpu.VMEM((K, HALF, B), F32), pltpu.VMEM((EARLY, 2, 8, HALF, NB), F32)]
    return pl.pallas_call(
        kernel,
        name="source_prepare",
        in_specs=[hbm] * 3,
        out_specs=[VMEM] * (5 + EARLY),
        out_shape=part_shapes() + rest,
        scratch_shapes=[
            pltpu.VMEM((R, B, NB), F32),
            pltpu.VMEM((B, K, NB), F32),
            pltpu.VMEM((EARLY, K, 2 * K, NB), F32),
            pltpu.VMEM((K, B, NB), F32),
            pltpu.SemaphoreType.DMA((8,)),
            pltpu.SemaphoreType.DMA((4,)),
            pltpu.SemaphoreType.DMA((EARLY,)),
        ],
        compiler_params=pltpu.CompilerParams(vmem_limit_bytes=15 * MIB),
    )(*in_hbm(sources, source_interp, transfer))


def source_rest(rest, after):
    def kernel(us_ref, um_ref, ut_ref, _, s_ref, m_ref, *t_refs):
        def place(count, rest_ref, out_ref):
            @pl.loop(0, count // 8)
            def _(i):
                first = pl.multiple_of(i * 8, 8)
                for q in range(0, HALF, 8):
                    out_ref[q : q + 8, pl.ds(first, 8), :] = jnp.swapaxes(rest_ref[pl.ds(first, 8), q : q + 8, :], 0, 1)

        place(K, um_ref, m_ref)
        place(R, us_ref, s_ref)
        for i, out_ref in enumerate(t_refs):
            for half in range(2):
                for gh in range(2):
                    for q in range(0, PART, 8):
                        rows = [ut_ref[i, half, j, gh * PART + q : gh * PART + q + 8, :] for j in range(8)]
                        place_transfer(rows, out_ref, q, gh, 16 * half)

    return pl.pallas_call(
        kernel,
        name="source_rest",
        in_specs=[VMEM] * 3 + [ANY],
        out_specs=[VMEM] * (2 + EARLY),
        out_shape=part_shapes(),
        compiler_params=pltpu.CompilerParams(vmem_limit_bytes=2 * MIB),
        cost_estimate=NEAR_ZERO,
    )(*in_vmem(*rest, after))


def source_stage(prepared, first, size, after):
    def kernel(s_ref, m_ref, t0_ref, t1_ref, _, o_ref, c_ref, d_ref):
        mask = low_lanes((K, NB))
        dims = (((1,), (1,)), ((), ()))
        for j in range(size):
            q = first % PART + j
            mh, ml = split(jnp.concatenate([m_ref[q], m_ref[q + PART]], 0))
            sh, sl = split(jnp.concatenate([s_ref[q], s_ref[q + PART]], 0))
            s = lax.dot_general(jnp.concatenate([mh, ml], 1), jnp.concatenate([sh, sh], 1), dims, preferred_element_type=F32)
            s = s + lax.dot_general(mh, sl, dims, preferred_element_type=F32)
            c_ref[j] = jnp.where(mask, s[:K], s[K:])
        for j in range(size):
            d_ref[j] = mix(t0_ref[first % PART + j], c_ref[j], c_ref[j ^ 1], mask)
        for j in range(size):
            o_ref[j] = mix(t1_ref[first % PART + j], d_ref[j], d_ref[j ^ 2], mask)

    return pl.pallas_call(
        kernel,
        name=f"source_{first}",
        in_specs=[VMEM] * 4 + [ANY],
        out_specs=VMEM,
        out_shape=pltpu.VMEM((size, K, NB), F32),
        scratch_shapes=[pltpu.VMEM((size, K, NB), F32)] * 2,
        compiler_params=pltpu.CompilerParams(vmem_limit_bytes=4 * MIB),
        cost_estimate=NEAR_ZERO,
    )(*in_vmem(*prepared, after))


def transfer_stage(transfer, level, after):
    def kernel(t_ref, _, o_ref):
        for i in range(2):
            prepare_transfer(t_ref.at[level, pl.ds(16 * i, 16)], o_ref, 16 * i)

    return pl.pallas_call(
        kernel,
        name=f"transfer_{level}",
        in_specs=[VMEM, ANY],
        out_specs=VMEM,
        out_shape=pltpu.VMEM((HALF, 2 * K, NB), BF16),
        compiler_params=pltpu.CompilerParams(vmem_limit_bytes=4 * MIB),
        cost_estimate=NEAR_ZERO,
    )(*in_vmem(transfer, after))


def target_matrix_kernel(ti_ref, _, o_ref, a_ref):
    for b0 in range(0, B, 8):
        a_ref[:, b0 : b0 + 8, :] = jnp.swapaxes(ti_ref[b0 : b0 + 8], 0, 1)

    @pl.loop(0, K // 8, unroll=True)
    def _(i):
        k0 = pl.multiple_of(i * 8, 8)
        turned = [a_ref[k0 + j].T for j in range(8)]
        for g0 in range(0, NB, 8):
            v = jnp.swapaxes(jnp.stack([t[g0 : g0 + 8] for t in turned]), 0, 1)
            o_ref[g0 : g0 + 8, pl.ds(k0, 8), :] = v


def target_matrix_stage(target_interp, after):
    return pl.pallas_call(
        target_matrix_kernel,
        name="target_matrix",
        in_specs=[VMEM, ANY],
        out_specs=VMEM,
        out_shape=pltpu.VMEM((NB, K, B), F32),
        scratch_shapes=[pltpu.VMEM((K, B, NB), F32)],
        compiler_params=pltpu.CompilerParams(vmem_limit_bytes=6 * MIB),
        cost_estimate=NEAR_ZERO,
    )(*in_vmem(target_interp, after))


def level_stage(weights, own, partner, first, level, after):
    size = own.shape[0]
    start = first % weights.shape[0]

    def kernel(t_ref, c_ref, p_ref, _, o_ref):
        mask = low_lanes((K, NB))
        for j in range(size):
            o_ref[j] = mix(t_ref[start + j], c_ref[j], p_ref[j], mask)

    return pl.pallas_call(
        kernel,
        name=f"level_{level}_{first}",
        in_specs=[VMEM] * 3 + [ANY],
        out_specs=VMEM,
        out_shape=pltpu.VMEM((size, K, NB), F32),
        compiler_params=pltpu.CompilerParams(vmem_limit_bytes=2 * MIB),
        cost_estimate=NEAR_ZERO,
    )(*in_vmem(weights, own, partner, after))


def last_stage(weights, own, partner, matrix, first, after):
    size = own.shape[0]

    def kernel(t_ref, c_ref, p_ref, m_ref, _, o_ref, d_ref, v_ref):
        mask = low_lanes((K, NB))
        for j in range(size):
            d_ref[j] = mix(t_ref[first + j], c_ref[j], p_ref[j], mask)
        for j in range(size):
            gl = first + j
            high, low = split(d_ref[j])
            left = jnp.concatenate([high, low, high, low], 0).T
            for gh in range(2):
                th, tl = split(m_ref[gh * HALF + gl])
                right = jnp.concatenate([th, th, tl, tl], 0)
                v_ref[gh, j] = jnp.dot(left[gh * R : gh * R + R], right, preferred_element_type=F32)
        for gh in range(2):
            for j0 in range(0, size, 8):
                for r0 in range(0, R, 8):
                    o_ref[r0 : r0 + 8, gh, j0 : j0 + 8, :] = jnp.swapaxes(v_ref[gh, j0 : j0 + 8, r0 : r0 + 8, :], 0, 1)

    return pl.pallas_call(
        kernel,
        name=f"last_{first}",
        in_specs=[VMEM] * 4 + [ANY],
        out_specs=VMEM,
        out_shape=pltpu.VMEM((R, 2, size, B), F32),
        scratch_shapes=[pltpu.VMEM((size, K, NB), F32), pltpu.VMEM((2, size, R, B), F32)],
        compiler_params=pltpu.CompilerParams(vmem_limit_bytes=4 * MIB),
        cost_estimate=NEAR_ZERO,
    )(*in_vmem(weights, own, partner, matrix, after))


def output_stage(parts):
    def kernel(*refs):
        ins, (o_hbm, o_ref, sem) = refs[:-3], refs[-3:]

        def copy(i):
            rows = pl.ds(pl.multiple_of(8 * i, 8), 8)
            return pltpu.make_async_copy(o_ref.at[rows], o_hbm.at[rows], sem.at[i])

        @pl.loop(0, 8, unroll=True)
        def _(i):
            for j in range(8):
                r = i * 8 + j
                o_ref[r] = jnp.concatenate([ref[r, gh] for gh in range(2) for ref in ins], 0).T
            copy(i).start()

        @pl.loop(0, 8, unroll=True)
        def _(i):
            copy(i).wait()

    return pl.pallas_call(
        kernel,
        name="output",
        in_specs=[VMEM] * len(parts),
        out_specs=pl.BlockSpec(memory_space=pltpu.HBM),
        out_shape=pltpu.HBM((R, B, NB), F32),
        scratch_shapes=[pltpu.VMEM((R, B, NB), F32), pltpu.SemaphoreType.DMA((8,))],
        compiler_params=pltpu.CompilerParams(vmem_limit_bytes=6 * MIB),
    )(*in_vmem(*parts))


def device_program(exchange, sources, source_interp, target_interp, transfer):
    prepared = source_prepare(sources, source_interp, transfer)
    count = len(CHUNKS)
    firsts = [sum(CHUNKS[:i]) for i in range(count)]
    early = [prepared[: 2 + EARLY], None]
    weights, parts = {}, {}
    level, own, partner = [1] * count, [None] * count, [None] * count
    after = prepared[2]
    for kind, index in ORDER:
        if kind == "prepare":
            if index == 1:
                early[1] = source_rest(prepared[2 + EARLY :], after)
                after = early[1][2]
            elif index == 9:
                after = weights[9] = target_matrix_stage(target_interp, after)
            else:
                after = weights[index] = transfer_stage(transfer, index, after)
            continue
        first, size, n = firsts[index], CHUNKS[index], level[index]
        if n == 8:
            after = parts[index] = last_stage(weights[8], own[index], partner[index], weights[9], first, after)
            continue
        if n == 1:
            after = source_stage(early[first // PART][:4], first, size, after)
        elif n == 2:
            after = level_stage(early[first // PART][4], own[index], partner[index], first, n, after)
        else:
            after = level_stage(weights[n], own[index], partner[index], first, n, after)
        own[index], level[index] = after, n + 1
        partner[index] = exchange(after, n + 1)
    return output_stage([parts[i] for i in range(count)])


def solution(mesh):
    n_src, n_tgt = mesh.shape["src"], mesh.shape["tgt"]

    def exchange(c, level):
        if level < 6:
            axis, size, bit = "src", n_src, level - 2
        else:
            axis, size, bit = "tgt", n_tgt, level - 6
        return lax.ppermute(c, axis, [(i, i ^ (1 << bit)) for i in range(size)])

    def program(*args):
        return device_program(exchange, *args)

    blocks = ("src", "tgt")
    return jax.shard_map(
        program,
        mesh=mesh,
        in_specs=(P(None, None, blocks), P(None, None, blocks), P(None, None, blocks), P(None, None, None, blocks)),
        out_specs=P(None, None, blocks),
        check_vma=False,
    )
```

```python
import jax
import jax.numpy as jnp
from jax import lax
from jax.experimental import pallas as pl
from jax.experimental.pallas import tpu as pltpu
from jax.sharding import PartitionSpec as P

R, B, K, NB = 64, 128, 32, 128
HALF = NB // 2
CHUNKS = (16, 16, 16, 16)
MIB = 1 << 20
F32, BF16 = jnp.float32, jnp.bfloat16
VMEM = pl.BlockSpec(memory_space=pltpu.VMEM)
ANY = pl.BlockSpec(memory_space=pl.ANY)
NEAR_ZERO = pl.CostEstimate(flops=1, bytes_accessed=1, transcendentals=0)
STEP = (0, 1, 0, 1, -1, -3, -4, -5, -6, -7, 0, 2, 1, 3, -8, 0, 2, 1, 3, 0, 2, 1, -9, 3, 0, 1, 2, 3, 0, 2, 1, 3, 2, 3, 0, 2, 1, 3, 2, 3)
ORDER = [("step", i) if i >= 0 else ("prepare", -i) for i in STEP]


def in_vmem(*arrays):
    return [pltpu.with_memory_space_constraint(x, pltpu.VMEM) for x in arrays]


def in_hbm(*arrays):
    return [pltpu.with_memory_space_constraint(x, pltpu.HBM) for x in arrays]


def split(x):
    high = x.astype(BF16)
    return high, (x - high.astype(F32)).astype(BF16)


def low_lanes(shape):
    return lax.broadcasted_iota(jnp.int32, shape, len(shape) - 1) < HALF


def turn_transfer(block):
    return [jnp.concatenate([block[i], block[i + 8]], 0).T for i in range(8)]


def place_transfer(turned, out_ref, gl, gh, k0):
    mask = low_lanes((8, 8, NB))
    v = jnp.swapaxes(jnp.stack(turned), 0, 1)
    w = pltpu.roll(v, HALF, 2)
    vh = v.astype(BF16).astype(F32)
    wh = w.astype(BF16).astype(F32)
    first = jnp.where(mask, vh, w - wh)
    second = jnp.where(mask, wh, v - vh)
    rows = jnp.concatenate([first, second], 1).astype(BF16)
    out_ref[gl : gl + 8, gh * K + k0 : gh * K + k0 + 16, :] = rows


def prepare_transfer(block, out_ref, k0):
    turned = turn_transfer(block)
    for g0 in range(0, NB, 8):
        gh, gl = divmod(g0, HALF)
        place_transfer([t[g0 : g0 + 8] for t in turned], out_ref, gl, gh, k0)


def mix(weight, own, partner, mask):
    high, low = split(jnp.concatenate([own, partner], 0))
    both = jnp.concatenate([weight, weight], 1)
    s = jnp.dot(both, jnp.concatenate([high, high, low, low], 0), preferred_element_type=F32)
    return jnp.where(mask, s[:K], s[K:])


PART = HALF // 2
EARLY = 3


def part_shapes():
    matrices = [pltpu.VMEM((PART, 2 * K, NB), BF16)] * EARLY
    return [pltpu.VMEM((HALF, R, B), F32), pltpu.VMEM((HALF, K, B), F32)] + matrices


def source_prepare(sources, source_interp, transfer):
    def kernel(src_hbm, si_hbm, t_hbm, s_ref, m_ref, *refs):
        t_refs, (us_ref, um_ref, ut_ref, src, si, t, a_ref, src_sem, si_sem, t_sem) = refs[:EARLY], refs[EARLY:]
        si_copy = [pltpu.make_async_copy(si_hbm.at[pl.ds(32 * i, 32)], si.at[pl.ds(32 * i, 32)], si_sem.at[i]) for i in range(4)]
        t_copy = [pltpu.make_async_copy(t_hbm.at[i], t.at[i], t_sem.at[i]) for i in range(EARLY)]

        def src_copy(i):
            rows = pl.ds(pl.multiple_of(8 * i, 8), 8)
            return pltpu.make_async_copy(src_hbm.at[rows], src.at[rows], src_sem.at[i])

        for copy in si_copy + [src_copy(i) for i in range(8)] + t_copy:
            copy.start()
        for i in range(4):
            si_copy[i].wait()
            for b0 in range(32 * i, 32 * i + 32, 8):
                a_ref[:, b0 : b0 + 8, :] = jnp.swapaxes(si[b0 : b0 + 8], 0, 1)

        def turn(block, out_ref, rest_ref, first):
            turned = [block(j).T for j in range(8)]
            for gh in range(2):
                for q in range(0, PART, 8):
                    g0 = gh * HALF + q
                    rows = jnp.swapaxes(jnp.stack([x[g0 : g0 + 8] for x in turned]), 0, 1)
                    out_ref[gh * PART + q : gh * PART + q + 8, pl.ds(first, 8), :] = rows
                g0 = gh * HALF + PART
                for j in range(8):
                    rest_ref[first + j, gh * PART : gh * PART + PART, :] = turned[j][g0 : g0 + PART]

        @pl.loop(0, K // 8, unroll=True)
        def _(i):
            k0 = pl.multiple_of(i * 8, 8)
            turn(lambda j: a_ref[k0 + j], m_ref, um_ref, k0)

        @pl.loop(0, 8, unroll=True)
        def _(i):
            src_copy(i).wait()
            r0 = pl.multiple_of(i * 8, 8)
            turn(lambda j: src[r0 + j], s_ref, us_ref, r0)

        for i, out_ref in enumerate(t_refs):
            t_copy[i].wait()
            for half in range(2):
                turned = turn_transfer(t.at[i, pl.ds(16 * half, 16)])
                for gh in range(2):
                    for q in range(0, PART, 8):
                        g0 = gh * HALF + q
                        place_transfer([x[g0 : g0 + 8] for x in turned], out_ref, q, gh, 16 * half)
                    g0 = gh * HALF + PART
                    for j in range(8):
                        ut_ref[i, half, j, gh * PART : gh * PART + PART, :] = turned[j][g0 : g0 + PART]

    hbm = pl.BlockSpec(memory_space=pltpu.HBM)
    rest = [pltpu.VMEM((R, HALF, B), F32), pltpu.VMEM((K, HALF, B), F32), pltpu.VMEM((EARLY, 2, 8, HALF, NB), F32)]
    return pl.pallas_call(
        kernel,
        name="source_prepare",
        in_specs=[hbm] * 3,
        out_specs=[VMEM] * (5 + EARLY),
        out_shape=part_shapes() + rest,
        scratch_shapes=[
            pltpu.VMEM((R, B, NB), F32),
            pltpu.VMEM((B, K, NB), F32),
            pltpu.VMEM((EARLY, K, 2 * K, NB), F32),
            pltpu.VMEM((K, B, NB), F32),
            pltpu.SemaphoreType.DMA((8,)),
            pltpu.SemaphoreType.DMA((4,)),
            pltpu.SemaphoreType.DMA((EARLY,)),
        ],
        compiler_params=pltpu.CompilerParams(vmem_limit_bytes=15 * MIB),
    )(*in_hbm(sources, source_interp, transfer))


def source_rest(rest, after):
    def kernel(us_ref, um_ref, ut_ref, _, s_ref, m_ref, *t_refs):
        def place(count, rest_ref, out_ref):
            @pl.loop(0, count // 8)
            def _(i):
                first = pl.multiple_of(i * 8, 8)
                for q in range(0, HALF, 8):
                    out_ref[q : q + 8, pl.ds(first, 8), :] = jnp.swapaxes(rest_ref[pl.ds(first, 8), q : q + 8, :], 0, 1)

        place(K, um_ref, m_ref)
        place(R, us_ref, s_ref)
        for i, out_ref in enumerate(t_refs):
            for half in range(2):
                for gh in range(2):
                    for q in range(0, PART, 8):
                        rows = [ut_ref[i, half, j, gh * PART + q : gh * PART + q + 8, :] for j in range(8)]
                        place_transfer(rows, out_ref, q, gh, 16 * half)

    return pl.pallas_call(
        kernel,
        name="source_rest",
        in_specs=[VMEM] * 3 + [ANY],
        out_specs=[VMEM] * (2 + EARLY),
        out_shape=part_shapes(),
        compiler_params=pltpu.CompilerParams(vmem_limit_bytes=2 * MIB),
        cost_estimate=NEAR_ZERO,
    )(*in_vmem(*rest, after))


def source_stage(prepared, first, size, after):
    def kernel(s_ref, m_ref, t0_ref, t1_ref, _, o_ref, c_ref, d_ref):
        mask = low_lanes((K, NB))
        dims = (((1,), (1,)), ((), ()))
        for j in range(size):
            q = first % PART + j
            mh, ml = split(jnp.concatenate([m_ref[q], m_ref[q + PART]], 0))
            sh, sl = split(jnp.concatenate([s_ref[q], s_ref[q + PART]], 0))
            s = lax.dot_general(jnp.concatenate([mh, ml], 1), jnp.concatenate([sh, sh], 1), dims, preferred_element_type=F32)
            s = s + lax.dot_general(mh, sl, dims, preferred_element_type=F32)
            c_ref[j] = jnp.where(mask, s[:K], s[K:])
        for j in range(size):
            d_ref[j] = mix(t0_ref[first % PART + j], c_ref[j], c_ref[j ^ 1], mask)
        for j in range(size):
            o_ref[j] = mix(t1_ref[first % PART + j], d_ref[j], d_ref[j ^ 2], mask)

    return pl.pallas_call(
        kernel,
        name=f"source_{first}",
        in_specs=[VMEM] * 4 + [ANY],
        out_specs=VMEM,
        out_shape=pltpu.VMEM((size, K, NB), F32),
        scratch_shapes=[pltpu.VMEM((size, K, NB), F32)] * 2,
        compiler_params=pltpu.CompilerParams(vmem_limit_bytes=4 * MIB),
        cost_estimate=NEAR_ZERO,
    )(*in_vmem(*prepared, after))


def transfer_stage(transfer, level, after):
    def kernel(t_ref, _, o_ref):
        for i in range(2):
            prepare_transfer(t_ref.at[level, pl.ds(16 * i, 16)], o_ref, 16 * i)

    return pl.pallas_call(
        kernel,
        name=f"transfer_{level}",
        in_specs=[VMEM, ANY],
        out_specs=VMEM,
        out_shape=pltpu.VMEM((HALF, 2 * K, NB), BF16),
        compiler_params=pltpu.CompilerParams(vmem_limit_bytes=4 * MIB),
        cost_estimate=NEAR_ZERO,
    )(*in_vmem(transfer, after))


def target_matrix_kernel(ti_ref, _, o_ref, a_ref):
    for b0 in range(0, B, 8):
        a_ref[:, b0 : b0 + 8, :] = jnp.swapaxes(ti_ref[b0 : b0 + 8], 0, 1)

    @pl.loop(0, K // 8, unroll=True)
    def _(i):
        k0 = pl.multiple_of(i * 8, 8)
        turned = [a_ref[k0 + j].T for j in range(8)]
        for g0 in range(0, NB, 8):
            v = jnp.swapaxes(jnp.stack([t[g0 : g0 + 8] for t in turned]), 0, 1)
            o_ref[g0 : g0 + 8, pl.ds(k0, 8), :] = v


def target_matrix_stage(target_interp, after):
    return pl.pallas_call(
        target_matrix_kernel,
        name="target_matrix",
        in_specs=[VMEM, ANY],
        out_specs=VMEM,
        out_shape=pltpu.VMEM((NB, K, B), F32),
        scratch_shapes=[pltpu.VMEM((K, B, NB), F32)],
        compiler_params=pltpu.CompilerParams(vmem_limit_bytes=6 * MIB),
        cost_estimate=NEAR_ZERO,
    )(*in_vmem(target_interp, after))


def level_stage(weights, own, partner, first, level, after):
    size = own.shape[0]
    start = first % weights.shape[0]

    def kernel(t_ref, c_ref, p_ref, _, o_ref):
        mask = low_lanes((K, NB))
        for j in range(size):
            o_ref[j] = mix(t_ref[start + j], c_ref[j], p_ref[j], mask)

    return pl.pallas_call(
        kernel,
        name=f"level_{level}_{first}",
        in_specs=[VMEM] * 3 + [ANY],
        out_specs=VMEM,
        out_shape=pltpu.VMEM((size, K, NB), F32),
        compiler_params=pltpu.CompilerParams(vmem_limit_bytes=2 * MIB),
        cost_estimate=NEAR_ZERO,
    )(*in_vmem(weights, own, partner, after))


def last_stage(weights, own, partner, matrix, first, after):
    size = own.shape[0]

    def kernel(t_ref, c_ref, p_ref, m_ref, _, o_ref, d_ref, v_ref):
        mask = low_lanes((K, NB))
        for j in range(size):
            d_ref[j] = mix(t_ref[first + j], c_ref[j], p_ref[j], mask)
        for j in range(size):
            gl = first + j
            high, low = split(d_ref[j])
            left = jnp.concatenate([high, low, high, low], 0).T
            for gh in range(2):
                th, tl = split(m_ref[gh * HALF + gl])
                right = jnp.concatenate([th, th, tl, tl], 0)
                v_ref[gh, j] = jnp.dot(left[gh * R : gh * R + R], right, preferred_element_type=F32)
        for gh in range(2):
            for j0 in range(0, size, 8):
                for r0 in range(0, R, 8):
                    o_ref[r0 : r0 + 8, gh, j0 : j0 + 8, :] = jnp.swapaxes(v_ref[gh, j0 : j0 + 8, r0 : r0 + 8, :], 0, 1)

    return pl.pallas_call(
        kernel,
        name=f"last_{first}",
        in_specs=[VMEM] * 4 + [ANY],
        out_specs=VMEM,
        out_shape=pltpu.VMEM((R, 2, size, B), F32),
        scratch_shapes=[pltpu.VMEM((size, K, NB), F32), pltpu.VMEM((2, size, R, B), F32)],
        compiler_params=pltpu.CompilerParams(vmem_limit_bytes=4 * MIB),
        cost_estimate=NEAR_ZERO,
    )(*in_vmem(weights, own, partner, matrix, after))


def output_stage(parts):
    def kernel(*refs):
        ins, (o_hbm, o_ref, sem) = refs[:-3], refs[-3:]

        def copy(i):
            rows = pl.ds(pl.multiple_of(8 * i, 8), 8)
            return pltpu.make_async_copy(o_ref.at[rows], o_hbm.at[rows], sem.at[i])

        @pl.loop(0, 8, unroll=True)
        def _(i):
            for j in range(8):
                r = i * 8 + j
                o_ref[r] = jnp.concatenate([ref[r, gh] for gh in range(2) for ref in ins], 0).T
            copy(i).start()

        @pl.loop(0, 8, unroll=True)
        def _(i):
            copy(i).wait()

    return pl.pallas_call(
        kernel,
        name="output",
        in_specs=[VMEM] * len(parts),
        out_specs=pl.BlockSpec(memory_space=pltpu.HBM),
        out_shape=pltpu.HBM((R, B, NB), F32),
        scratch_shapes=[pltpu.VMEM((R, B, NB), F32), pltpu.SemaphoreType.DMA((8,))],
        compiler_params=pltpu.CompilerParams(vmem_limit_bytes=6 * MIB),
    )(*in_vmem(*parts))


def device_program(exchange, sources, source_interp, target_interp, transfer):
    prepared = source_prepare(sources, source_interp, transfer)
    count = len(CHUNKS)
    firsts = [sum(CHUNKS[:i]) for i in range(count)]
    early = [prepared[: 2 + EARLY], None]
    weights, parts = {}, {}
    level, own, partner = [1] * count, [None] * count, [None] * count
    after = prepared[2]
    for kind, index in ORDER:
        if kind == "prepare":
            if index == 1:
                early[1] = source_rest(prepared[2 + EARLY :], after)
                after = early[1][2]
            elif index == 9:
                after = weights[9] = target_matrix_stage(target_interp, after)
            else:
                after = weights[index] = transfer_stage(transfer, index, after)
            continue
        first, size, n = firsts[index], CHUNKS[index], level[index]
        if n == 8:
            after = parts[index] = last_stage(weights[8], own[index], partner[index], weights[9], first, after)
            continue
        if n == 1:
            after = source_stage(early[first // PART][:4], first, size, after)
        elif n == 2:
            after = level_stage(early[first // PART][4], own[index], partner[index], first, n, after)
        else:
            after = level_stage(weights[n], own[index], partner[index], first, n, after)
        own[index], level[index] = after, n + 1
        partner[index] = exchange(after, n + 1)
    return output_stage([parts[i] for i in range(count)])


def solution(mesh):
    n_src, n_tgt = mesh.shape["src"], mesh.shape["tgt"]

    def exchange(c, level):
        if level < 6:
            axis, size, bit = "src", n_src, level - 2
        else:
            axis, size, bit = "tgt", n_tgt, level - 6
        return lax.ppermute(c, axis, [(i, i ^ (1 << bit)) for i in range(size)])

    def program(*args):
        return device_program(exchange, *args)

    blocks = ("src", "tgt")
    return jax.shard_map(
        program,
        mesh=mesh,
        in_specs=(P(None, None, blocks), P(None, None, blocks), P(None, None, blocks), P(None, None, None, blocks)),
        out_specs=P(None, None, blocks),
        check_vma=False,
    )
```
